32 devices in a mesh: grp: 2 (over y), ka: 4 (over z), vib: 2 (over core), fin: 2 (over x).
Axes of the slice: x: 2, y: 2, z: 4, core: 2. Of those that a mesh axis runs over, the one named last changes fastest.
Arguments:
- moments: bfloat16 [2, 2048, 2048], P(None, 'vib'), may hold values from -0.125 to 0.125
- initial_vectors: bfloat16 [8, 2048, 2048], P('ka', 'vib', 'grp'), parts along dimension 2, may hold values from -6 to 6
- final_vectors: bfloat16 [8, 2048, 1024], P('ka', 'vib', ('grp', 'fin')), parts along dimension 2, may hold values from -0.046875 to 0.046875
- basis_counts: int32 [16], P(('grp', 'ka')), parts along dimension 0, may hold values from 512 to 2048
Outputs:
- strengths: float32 [2048, 512], P(('grp', 'ka', 'vib'), 'fin'), parts along dimension 0
The draws below stay inside these ranges and needn't reach their ends.
There are 2 independent parts, one for each index of `grp`. The reference program is written for one: setup_inputs(seed, part) draws one part's arguments, and reference() takes and returns one part's arrays. A program takes and returns all parts, laid end to end along the dimension named above; an argument that names none is the same for every part. Nothing has to cross between parts.
All inputs are finite; a program needn't handle non-finite values.
Results may differ from the reference program's by a relative error of at most 0.0003.
Values may be sent and summed in bfloat16 or wider, within the bound.
A program may use at most 64 MiB of HBM per device.

```python
import jax
import jax.numpy as jnp
from jax import lax

NV = 2048
NI = 1024
NF = 512
JQ = 30
KB = 8


def place_ends(entries, rng, least, largest):
    extent = entries.shape
    spot = [jax.random.randint(jax.random.fold_in(rng, axis), (), 0, extent[axis]) for axis in range(len(extent))]
    entries = entries.at[tuple(spot)].set(least)
    longest = extent.index(max(extent))
    spot[longest] = (spot[longest] + 1) % extent[longest]
    return entries.at[tuple(spot)].set(largest)


def block_scale(stream_key, extent, shards, smallest, top_value):
    def one(axis_at, shards_of):
        steps = jax.random.uniform(jax.random.fold_in(jax.random.fold_in(stream_key, 6), axis_at), (shards_of,), jnp.float32, smallest / len(shards), top_value / len(shards))
        return jnp.repeat(jnp.exp(steps), extent[axis_at] // shards_of).reshape((-1,) + (1,) * (len(extent) - axis_at - 1))

    loudness = one(*shards[0])
    for cut in shards[1:]:
        loudness = loudness * one(*cut)
    return loudness


def gaussian(key, shape, deviation, limit, shards=(), held_as=jnp.bfloat16):
    drawn = jax.random.normal(key, shape, jnp.float32) * deviation
    if len(shards) > 0:
        drawn = block_scale(key, shape, shards, -0.22, 0.18) * drawn
    return jnp.clip(drawn, min=-limit, max=limit).astype(held_as)


def setup_inputs(seed: int = 0, part: int = 0) -> dict:
    streams_of = jax.random.split(jax.random.key(seed), 5)
    own_keys = jax.random.split(jax.random.fold_in(streams_of[4], part), 5)
    return {
        "moments": gaussian(streams_of[0], (2, NV, NV), NV ** -0.5, 0.125, ((1, 2),)),
        "initial_vectors": gaussian(own_keys[1], (KB, NV, NI), 1.0, 6.0, ((0, 4), (1, 2))),
        "final_vectors": gaussian(own_keys[2], (KB, NV, NF), (NV * KB) ** -0.5, 0.046875, ((0, 4), (1, 2), (2, 2))),
        "basis_counts": place_ends(jax.random.randint(own_keys[3], (KB,), NV // 4, NV + 1), jax.random.fold_in(own_keys[3], 1), NV // 4, NV).astype(jnp.int32),
    }


def reference(moments, initial_vectors, final_vectors, basis_counts):
    row_index = jnp.arange(NV, dtype=jnp.int32)
    keep_mask = row_index[None, :] < basis_counts[:, None]
    initial_live = jnp.where(keep_mask[:, :, None], initial_vectors, jnp.zeros((), initial_vectors.dtype))
    final_live = jnp.where(keep_mask[:, :, None], final_vectors, jnp.zeros((), final_vectors.dtype))
    moment_f32 = moments.astype(jnp.float32)

    def project_block(eigen_block):
        return jnp.einsum('cvw,vi->cwi', moment_f32, eigen_block.astype(jnp.float32), precision=lax.Precision.HIGHEST)
    projected = lax.map(project_block, initial_live)
    jsquare = float(JQ * (JQ + 1))
    norm_j = jnp.sqrt(jnp.float32(jsquare))
    k_value = (jnp.arange(KB, dtype=jnp.int32) - KB // 2).astype(jnp.float32)
    coef_same = k_value / norm_j
    coef_upper = 0.5 * jnp.sqrt(jsquare - k_value * (k_value + 1.0)) / norm_j
    coef_lower = -0.5 * jnp.sqrt(jsquare - k_value * (k_value - 1.0)) / norm_j
    along_z = projected[:, 0]
    along_x = projected[:, 1]
    zero_block = jnp.zeros_like(along_x[:1])
    upper_x = jnp.concatenate([along_x[1:], zero_block], axis=0)
    lower_x = jnp.concatenate([zero_block, along_x[:-1]], axis=0)
    coupled = coef_same[:, None, None] * along_z + coef_upper[:, None, None] * upper_x + coef_lower[:, None, None] * lower_x
    amplitude = jnp.einsum('kvf,kvi->if', final_live.astype(jnp.float32), coupled, precision=lax.Precision.HIGHEST)
    return amplitude * amplitude
```

```python
import functools

import jax
import jax.numpy as jnp
from jax import lax
from jax.experimental import pallas as pl
from jax.experimental.pallas import tpu as pltpu
from jax.sharding import PartitionSpec as P

JQ = 30
MESH = pl.DeviceIdType.MESH
F32 = jnp.float32
BF16 = jnp.bfloat16


def coefficient_rows(index, width):
    value = jnp.full((1, width), index, jnp.int32).astype(F32)
    jsquare = float(JQ * (JQ + 1))
    norm_j = jnp.sqrt(jnp.full((1, width), jsquare, F32))
    same = value / norm_j
    upper = 0.5 * jnp.sqrt(jsquare - value * (value + 1.0)) / norm_j
    lower = -0.5 * jnp.sqrt(jsquare - value * (value - 1.0)) / norm_j
    return same, upper, lower


def kernel(
    n_ka, chunks, counts_ref, moments_hbm, initial_hbm, final_hbm, out_ref,
    mom, ini, raw, fin, comb, split, amp, part, zsend, zrecv,
    mom_sem, ini_sem, raw_sem, own_send, own_recv, z_send, z_recv,
    fwd_send, fwd_recv, part_send, part_recv, out_send, out_recv,
):
    kblocks, rows, width = raw.shape
    states = ini.shape[2]
    share = out_ref.shape[0]
    whole = mom.shape[2]
    total_blocks = kblocks * n_ka
    a = lax.axis_index("ka")
    b = lax.axis_index("vib")
    other = 1 - b
    first = a * kblocks - total_blocks // 2

    get_final = pltpu.make_async_copy(final_hbm, raw, raw_sem)
    get_final.start()
    tile = mom.shape[1] // mom_sem.shape[1]
    get_moments = []
    for t in range(mom_sem.shape[1]):
        for c in range(2):
            get_moments.append(
                pltpu.make_async_copy(
                    moments_hbm.at[c, pl.ds(t * tile, tile)],
                    mom.at[c, pl.ds(t * tile, tile)],
                    mom_sem.at[c, t],
                )
            )
            get_moments[-1].start()
    get_initial = pltpu.make_async_copy(initial_hbm, ini, ini_sem)
    get_initial.start()

    barrier = pltpu.get_barrier_semaphore()
    pl.semaphore_signal(barrier, inc=1, device_id={"vib": other}, device_id_type=MESH)
    for d in range(1, n_ka):
        pl.semaphore_signal(
            barrier, inc=1, device_id={"ka": lax.rem(a + d, n_ka)}, device_id_type=MESH
        )

    get_final.wait()
    own_rows = pl.ds(pl.multiple_of(b * rows, rows), rows)
    row_index = lax.broadcasted_iota(jnp.int32, (rows, width), 0) + b * rows
    for k in range(kblocks):
        live = row_index < counts_ref[k]
        fin[1 + k, own_rows, :] = jnp.where(live, raw[k].astype(F32), 0.0).astype(BF16)

    has_up = a < n_ka - 1
    has_down = a > 0
    pl.semaphore_wait(barrier, n_ka)

    step = rows // chunks

    def at(core, j):
        return pl.ds(pl.multiple_of(core * rows + j * step, step), step)

    def z_copy(side, j):
        src, dst, to = (2, 0, a + 1) if side == 0 else (1, 3, a - 1)
        return pltpu.make_async_remote_copy(
            src_ref=fin.at[src, at(b, j)],
            dst_ref=fin.at[dst, at(b, j)],
            send_sem=z_send.at[side, j],
            recv_sem=z_recv.at[side, j],
            device_id={"ka": to},
            device_id_type=MESH,
        )

    def forward(side, j):
        slot = 0 if side == 0 else 3
        return pltpu.make_async_remote_copy(
            src_ref=fin.at[slot, at(b, j)],
            dst_ref=fin.at[slot, at(b, j)],
            send_sem=fwd_send.at[side, j],
            recv_sem=fwd_recv.at[side, j],
            device_id={"vib": other},
            device_id_type=MESH,
        )

    sends = (has_up, has_down)
    takes = (has_down, has_up)
    for j in range(chunks):
        for side in range(2):
            @pl.when(sends[side])
            def _():
                z_copy(side, j).start()
    own = pltpu.make_async_remote_copy(
        src_ref=fin.at[pl.ds(1, kblocks), own_rows],
        dst_ref=fin.at[pl.ds(1, kblocks), own_rows],
        send_sem=own_send,
        recv_sem=own_recv,
        device_id={"vib": other},
        device_id_type=MESH,
    )
    own.start()
    for side in range(2):
        @pl.when(jnp.logical_not(takes[side]))
        def _():
            fin[3 * side] = jnp.zeros((whole, width), BF16)

    same0, upper0, _ = coefficient_rows(first, width)
    same1, _, lower1 = coefficient_rows(first + 1, width)
    _, upper_below, _ = coefficient_rows(first - 1, width)
    _, _, lower_above = coefficient_rows(first + 2, width)

    own.wait_recv()
    for t in range(mom_sem.shape[1]):
        get_moments[2 * t].wait()
        get_moments[2 * t + 1].wait()
        span = pl.ds(t * tile, tile)
        z_part = functools.partial(jnp.dot, mom[0, span, :], preferred_element_type=F32)
        x_part = functools.partial(jnp.dot, mom[1, span, :], preferred_element_type=F32)
        comb[0, span, :] = same0 * z_part(fin[1]) + lower1 * x_part(fin[2])
        comb[1, span, :] = same1 * z_part(fin[2]) + upper0 * x_part(fin[1])

    edge = (upper_below, lower_above)

    def take(side, core, j):
        piece = fin[3 * side, at(core, j), :]
        cols = pl.ds(pl.multiple_of(core * rows + j * step, step), step)
        comb[side] = comb[side] + edge[side] * jnp.dot(
            mom[1, :, cols], piece, preferred_element_type=F32
        )

    for j in range(chunks):
        for side in range(2):
            @pl.when(takes[side])
            def _():
                z_copy(side, j).wait_recv()
                forward(side, j).start()
        for side in range(2):
            take(side, b, j)
        for side in range(2):
            @pl.when(takes[side])
            def _():
                forward(side, j).wait_recv()
        for side in range(2):
            take(side, other, j)

    block = min(256, rows)
    lane_index = lax.broadcasted_iota(jnp.int32, (width, block), 1) + b * rows
    for k in range(kblocks):
        for t in range(rows // block):
            turned = comb[k, pl.ds(t * block, block), :].T
            turned = jnp.where(lane_index + t * block < counts_ref[k], turned, 0.0)
            high = turned.astype(BF16)
            low = (turned - high.astype(F32)).astype(BF16)
            split[k, pl.ds(0, width), pl.ds(t * block, block)] = high
            split[k, pl.ds(width, width), pl.ds(t * block, block)] = low

    get_initial.wait()
    lanes = min(256, states)
    n_blocks = states // lanes
    targets = lanes // (2 * share)
    own_block = a // targets if targets > 1 else a

    def block_of(s):
        return lax.rem(own_block + 1 + s, n_blocks)

    def part_copy(s):
        span = pl.ds(pl.multiple_of(block_of(s) * (targets * share), targets * share), targets * share)
        return pltpu.make_async_remote_copy(
            src_ref=amp.at[other, span],
            dst_ref=part.at[span],
            send_sem=part_send.at[s],
            recv_sem=part_recv.at[s],
            device_id={"vib": other},
            device_id_type=MESH,
        )

    def out_copy(target, slot):
        return pltpu.make_async_remote_copy(
            src_ref=zsend.at[slot],
            dst_ref=zrecv.at[a],
            send_sem=out_send.at[slot],
            recv_sem=out_recv.at[a],
            device_id={"ka": target},
            device_id_type=MESH,
        )

    def finish(s):
        part_copy(s).wait_recv()
        for j in range(targets):
            target = block_of(s) * targets + j
            span = pl.ds(pl.multiple_of(target * share, share), share)
            slot = s * targets + j
            value = amp[b, span, :] + part[span, :]
            zsend[slot] = value

            @pl.when(target == a)
            def _():
                out_ref[...] = value

            @pl.when(target != a)
            def _():
                out_copy(target, slot).start()

    for s in range(n_blocks):
        cols = pl.ds(pl.multiple_of(block_of(s) * lanes, lanes), lanes)
        both = jnp.dot(split[0], ini[0, :, cols], preferred_element_type=F32)
        for k in range(1, kblocks):
            both = both + jnp.dot(split[k], ini[k, :, cols], preferred_element_type=F32)
        value = (both[:width] + both[width:]).T
        for j in range(targets):
            for core in range(2):
                low = (j * 2 + core) * share
                target = block_of(s) * targets + j
                amp[core, pl.ds(pl.multiple_of(target * share, share), share), :] = value[
                    low : low + share
                ]
        part_copy(s).start()
        if s > 0:
            finish(s - 1)
    finish(n_blocks - 1)

    for d in range(1, n_ka):
        sender = lax.rem(a + d, n_ka)
        pltpu.make_async_remote_copy(
            src_ref=zsend.at[0],
            dst_ref=zrecv.at[sender],
            send_sem=out_send.at[0],
            recv_sem=out_recv.at[sender],
            device_id={"ka": sender},
            device_id_type=MESH,
        ).wait_recv()
        out_ref[...] = out_ref[...] + zrecv[sender]

    own.wait_send()
    for j in range(chunks):
        for side in range(2):
            @pl.when(sends[side])
            def _():
                z_copy(side, j).wait_send()

            @pl.when(takes[side])
            def _():
                forward(side, j).wait_send()
    for s in range(n_blocks):
        part_copy(s).wait_send()
        for j in range(targets):
            target = block_of(s) * targets + j

            @pl.when(target != a)
            def _():
                out_copy(target, s * targets + j).wait_send()


def on_device(n_ka, moments, initial_vectors, final_vectors, basis_counts):
    kblocks, rows, states = initial_vectors.shape
    width = final_vectors.shape[2]
    whole = moments.shape[2]
    share = states // (2 * n_ka)
    chunks = 4
    tiles = 2
    dma = pltpu.SemaphoreType.DMA
    n_blocks = states // min(256, states)
    amplitude = pl.pallas_call(
        functools.partial(kernel, n_ka, chunks),
        out_shape=jax.ShapeDtypeStruct((share, width), F32),
        in_specs=[pl.BlockSpec(memory_space=pltpu.SMEM)]
        + [pl.BlockSpec(memory_space=pl.ANY)] * 3,
        out_specs=pl.BlockSpec(memory_space=pltpu.VMEM),
        scratch_shapes=[
            pltpu.VMEM(moments.shape, BF16),
            pltpu.VMEM(initial_vectors.shape, BF16),
            pltpu.VMEM(final_vectors.shape, BF16),
            pltpu.VMEM((kblocks + 2, whole, width), BF16),
            pltpu.VMEM((kblocks, rows, width), F32),
            pltpu.VMEM((kblocks, 2 * width, rows), BF16),
            pltpu.VMEM((2, n_ka * share, width), F32),
            pltpu.VMEM((n_ka * share, width), F32),
            pltpu.VMEM((n_ka, share, width), F32),
            pltpu.VMEM((n_ka, share, width), F32),
            dma((2, tiles)),
            dma(()),
            dma(()),
            dma(()),
            dma(()),
            dma((2, chunks)),
            dma((2, chunks)),
            dma((2, chunks)),
            dma((2, chunks)),
            dma((n_blocks,)),
            dma((n_blocks,)),
            dma((n_ka,)),
            dma((n_ka,)),
        ],
        compiler_params=pltpu.CompilerParams(
            collective_id=0, has_side_effects=True, vmem_limit_bytes=60 * 2**20
        ),
    )(basis_counts, moments, initial_vectors, final_vectors)
    return amplitude * amplitude


def solution(mesh):
    in_specs = (
        P(None, "vib", None),
        P("ka", "vib", "grp"),
        P("ka", "vib", ("grp", "fin")),
        P(("grp", "ka")),
    )
    out_specs = P(("grp", "ka", "vib"), "fin")
    return jax.shard_map(
        functools.partial(on_device, mesh.shape["ka"]),
        mesh=mesh, in_specs=in_specs, out_specs=out_specs, check_vma=False,
    )
```

```python
import functools

import jax
import jax.numpy as jnp
from jax import lax
from jax.experimental import pallas as pl
from jax.experimental.pallas import tpu as pltpu
from jax.sharding import PartitionSpec as P

JQ = 30
MESH = pl.DeviceIdType.MESH
F32 = jnp.float32
BF16 = jnp.bfloat16


def coefficient_rows(index, width):
    value = jnp.full((1, width), index, jnp.int32).astype(F32)
    jsquare = float(JQ * (JQ + 1))
    norm_j = jnp.sqrt(jnp.full((1, width), jsquare, F32))
    same = value / norm_j
    upper = 0.5 * jnp.sqrt(jsquare - value * (value + 1.0)) / norm_j
    lower = -0.5 * jnp.sqrt(jsquare - value * (value - 1.0)) / norm_j
    return same, upper, lower


def kernel(
    n_ka, n_half, chunks, counts_ref, moments_hbm, initial_hbm, final_hbm, out_ref,
    mom, ini, raw, own, edge, comb, split, amp, part, zsend, zrecv,
    mom_sem, ini_sem, raw_sem, own_send, own_recv, z_send, z_recv,
    fwd_send, fwd_recv, part_send, part_recv, out_send, out_recv,
):
    kblocks, rows, width = raw.shape
    states = ini.shape[2]
    share = out_ref.shape[0]
    whole = mom.shape[2]
    half = width // n_half
    a = lax.axis_index("ka")
    b = lax.axis_index("vib")
    other = 1 - b
    first = a * kblocks - kblocks * n_ka // 2

    get_final = pltpu.make_async_copy(final_hbm, raw, raw_sem)
    get_final.start()
    cores = (b, other)

    def cols_of(core):
        return pl.ds(pl.multiple_of(core * rows, rows), rows)

    def get_moments(i, c):
        span = cols_of(cores[i])
        return pltpu.make_async_copy(
            moments_hbm.at[c, :, span], mom.at[c, :, span], mom_sem.at[i, c]
        )

    for i in range(2):
        for c in range(2):
            get_moments(i, c).start()
    get_initial = pltpu.make_async_copy(initial_hbm, ini, ini_sem)
    get_initial.start()

    barrier = pltpu.get_barrier_semaphore()
    pl.semaphore_signal(barrier, inc=1, device_id={"vib": other}, device_id_type=MESH)
    for d in range(1, n_ka):
        pl.semaphore_signal(
            barrier, inc=1, device_id={"ka": lax.rem(a + d, n_ka)}, device_id_type=MESH
        )

    get_final.wait()
    own_rows = cols_of(b)
    row_index = lax.broadcasted_iota(jnp.int32, (rows, half), 0) + b * rows
    for h in range(n_half):
        for k in range(kblocks):
            live = row_index < counts_ref[k]
            piece = raw[k, :, h * half : (h + 1) * half].astype(F32)
            own[h, own_rows, k * half : (k + 1) * half] = jnp.where(live, piece, 0.0).astype(BF16)

    has_up = a < n_ka - 1
    has_down = a > 0
    pl.semaphore_wait(barrier, n_ka)

    step = rows // chunks

    def at(core, j):
        return pl.ds(pl.multiple_of(core * rows + j * step, step), step)

    def side_lanes(side):
        return pl.ds(side * half, half)

    def z_copy(side, h, j):
        to = a + 1 if side == 0 else a - 1
        return pltpu.make_async_remote_copy(
            src_ref=own.at[h, at(b, j), side_lanes(1 - side)],
            dst_ref=edge.at[h, at(b, j), side_lanes(side)],
            send_sem=z_send.at[side, h, j],
            recv_sem=z_recv.at[side, h, j],
            device_id={"ka": to},
            device_id_type=MESH,
        )

    def forward(side, h, j):
        return pltpu.make_async_remote_copy(
            src_ref=edge.at[h, at(b, j), side_lanes(side)],
            dst_ref=edge.at[h, at(b, j), side_lanes(side)],
            send_sem=fwd_send.at[side, h, j],
            recv_sem=fwd_recv.at[side, h, j],
            device_id={"vib": other},
            device_id_type=MESH,
        )

    def own_copy(h):
        return pltpu.make_async_remote_copy(
            src_ref=own.at[h, own_rows],
            dst_ref=own.at[h, own_rows],
            send_sem=own_send.at[h],
            recv_sem=own_recv.at[h],
            device_id={"vib": other},
            device_id_type=MESH,
        )

    sends = (has_up, has_down)
    takes = (has_down, has_up)
    for h in range(n_half):
        for j in range(chunks):
            for side in range(2):
                @pl.when(sends[side])
                def _():
                    z_copy(side, h, j).start()
        own_copy(h).start()
    for side in range(2):
        @pl.when(jnp.logical_not(takes[side]))
        def _():
            for h in range(n_half):
                edge[h, :, side * half : (side + 1) * half] = jnp.zeros((whole, half), BF16)

    same0, upper0, _ = coefficient_rows(first, half)
    same1, _, lower1 = coefficient_rows(first + 1, half)
    _, upper_below, _ = coefficient_rows(first - 1, half)
    _, _, lower_above = coefficient_rows(first + 2, half)
    same_row = jnp.concatenate([same0, same1], axis=1)
    cross_row = jnp.concatenate([lower1, upper0], axis=1)
    edge_row = jnp.concatenate([upper_below, lower_above], axis=1)

    def relay(h, j):
        for side in range(2):
            @pl.when(takes[side])
            def _():
                z_copy(side, h, j).wait_recv()
                forward(side, h, j).start()

    tile = rows // 2
    for i in range(2):
        for c in range(2):
            get_moments(i, c).wait()
        for h in range(n_half):
            if i == 1:
                own_copy(h).wait_recv()
            piece = own[h, cols_of(cores[i]), :]
            for t in range(2):
                span = pl.ds(t * tile, tile)
                along_z = jnp.dot(
                    mom[0, span, cols_of(cores[i])], piece, preferred_element_type=F32
                )
                along_x = jnp.dot(
                    mom[1, span, cols_of(cores[i])], piece, preferred_element_type=F32
                )
                crossed = jnp.concatenate([along_x[:, half:], along_x[:, :half]], axis=1)
                value = same_row * along_z + cross_row * crossed
                comb[h, span, :] = value if i == 0 else comb[h, span, :] + value

    def take(h, core, j):
        piece = edge[h, at(core, j), :]
        for t in range(2):
            span = pl.ds(t * tile, tile)
            comb[h, span, :] = comb[h, span, :] + edge_row * jnp.dot(
                mom[1, span, at(core, j)], piece, preferred_element_type=F32
            )

    block = min(256, rows)
    lane_index = lax.broadcasted_iota(jnp.int32, (half, block), 1) + b * rows

    def split_half(h):
        for t in range(rows // block):
            both = comb[h, pl.ds(t * block, block), :].T
            for k in range(kblocks):
                turned = both[k * half : (k + 1) * half]
                turned = jnp.where(lane_index + t * block < counts_ref[k], turned, 0.0)
                high = turned.astype(BF16)
                low = (turned - high.astype(F32)).astype(BF16)
                split[h, k, pl.ds(0, half), pl.ds(t * block, block)] = high
                split[h, k, pl.ds(half, half), pl.ds(t * block, block)] = low

    lanes = min(256, states)
    n_blocks = states // lanes
    targets = lanes // (2 * share)
    own_block = a // targets if targets > 1 else a

    def block_of(s):
        return lax.rem(own_block + 1 + s, n_blocks)

    def part_copy(h, s):
        size = targets * share
        span = pl.ds(pl.multiple_of(block_of(s) * size, size), size)
        return pltpu.make_async_remote_copy(
            src_ref=amp.at[h, other, span],
            dst_ref=part.at[h, span],
            send_sem=part_send.at[h, s],
            recv_sem=part_recv.at[h, s],
            device_id={"vib": other},
            device_id_type=MESH,
        )

    def out_copy(h, target, slot):
        return pltpu.make_async_remote_copy(
            src_ref=zsend.at[h, slot],
            dst_ref=zrecv.at[h, a],
            send_sem=out_send.at[h, slot],
            recv_sem=out_recv.at[h, a],
            device_id={"ka": target},
            device_id_type=MESH,
        )

    def finish(h, s):
        part_copy(h, s).wait_recv()
        for j in range(targets):
            target = block_of(s) * targets + j
            span = pl.ds(pl.multiple_of(target * share, share), share)
            slot = s * targets + j
            value = amp[h, b, span, :] + part[h, span, :]
            zsend[h, slot] = value

            @pl.when(target == a)
            def _():
                out_ref[:, h * half : (h + 1) * half] = value

            @pl.when(target != a)
            def _():
                out_copy(h, target, slot).start()

    def amplitude_block(h, s):
        cols = pl.ds(pl.multiple_of(block_of(s) * lanes, lanes), lanes)
        both = jnp.dot(split[h, 0], ini[0, :, cols], preferred_element_type=F32)
        for k in range(1, kblocks):
            both = both + jnp.dot(split[h, k], ini[k, :, cols], preferred_element_type=F32)
        value = (both[:half] + both[half:]).T
        for j in range(targets):
            for core in range(2):
                low = (j * 2 + core) * share
                target = block_of(s) * targets + j
                amp[h, core, pl.ds(pl.multiple_of(target * share, share), share), :] = value[
                    low : low + share
                ]
        part_copy(h, s).start()

    for h in range(n_half):
        for j in range(chunks):
            if h == 0 or j > 0:
                relay(h, j)
            take(h, b, j)
        for j in range(chunks):
            for side in range(2):
                @pl.when(takes[side])
                def _():
                    forward(side, h, j).wait_recv()
            take(h, other, j)
        split_half(h)
        if h == 0:
            get_initial.wait()
        for s in range(n_blocks):
            amplitude_block(h, s)
            if s > 0:
                finish(h, s - 1)
            if s == n_blocks // 2 and h + 1 < n_half:
                relay(h + 1, 0)
    for h in range(n_half):
        finish(h, n_blocks - 1)

    for h in range(n_half):
        for d in range(1, n_ka):
            sender = lax.rem(a + d, n_ka)
            pltpu.make_async_remote_copy(
                src_ref=zsend.at[h, 0],
                dst_ref=zrecv.at[h, sender],
                send_sem=out_send.at[h, 0],
                recv_sem=out_recv.at[h, sender],
                device_id={"ka": sender},
                device_id_type=MESH,
            ).wait_recv()
            lanes_h = pl.ds(h * half, half)
            out_ref[:, lanes_h] = out_ref[:, lanes_h] + zrecv[h, sender]

    for h in range(n_half):
        own_copy(h).wait_send()
        for j in range(chunks):
            for side in range(2):
                @pl.when(sends[side])
                def _():
                    z_copy(side, h, j).wait_send()

                @pl.when(takes[side])
                def _():
                    forward(side, h, j).wait_send()
        for s in range(n_blocks):
            part_copy(h, s).wait_send()
            for j in range(targets):
                target = block_of(s) * targets + j

                @pl.when(target != a)
                def _():
                    out_copy(h, target, s * targets + j).wait_send()


def on_device(n_ka, moments, initial_vectors, final_vectors, basis_counts):
    kblocks, rows, states = initial_vectors.shape
    width = final_vectors.shape[2]
    whole = moments.shape[2]
    share = states // (2 * n_ka)
    n_half = max(1, width // 128)
    half = width // n_half
    chunks = 2
    dma = pltpu.SemaphoreType.DMA
    n_blocks = states // min(256, states)
    amplitude = pl.pallas_call(
        functools.partial(kernel, n_ka, n_half, chunks),
        out_shape=jax.ShapeDtypeStruct((share, width), F32),
        in_specs=[pl.BlockSpec(memory_space=pltpu.SMEM)]
        + [pl.BlockSpec(memory_space=pl.ANY)] * 3,
        out_specs=pl.BlockSpec(memory_space=pltpu.VMEM),
        scratch_shapes=[
            pltpu.VMEM(moments.shape, BF16),
            pltpu.VMEM(initial_vectors.shape, BF16),
            pltpu.VMEM(final_vectors.shape, BF16),
            pltpu.VMEM((n_half, whole, kblocks * half), BF16),
            pltpu.VMEM((n_half, whole, 2 * half), BF16),
            pltpu.VMEM((n_half, rows, kblocks * half), F32),
            pltpu.VMEM((n_half, kblocks, 2 * half, rows), BF16),
            pltpu.VMEM((n_half, 2, n_ka * share, half), F32),
            pltpu.VMEM((n_half, n_ka * share, half), F32),
            pltpu.VMEM((n_half, n_ka, share, half), F32),
            pltpu.VMEM((n_half, n_ka, share, half), F32),
            dma((2, 2)),
            dma(()),
            dma(()),
            dma((n_half,)),
            dma((n_half,)),
            dma((2, n_half, chunks)),
            dma((2, n_half, chunks)),
            dma((2, n_half, chunks)),
            dma((2, n_half, chunks)),
            dma((n_half, n_blocks)),
            dma((n_half, n_blocks)),
            dma((n_half, n_ka)),
            dma((n_half, n_ka)),
        ],
        compiler_params=pltpu.CompilerParams(
            collective_id=0, has_side_effects=True, vmem_limit_bytes=60 * 2**20
        ),
    )(basis_counts, moments, initial_vectors, final_vectors)
    return amplitude * amplitude


def solution(mesh):
    in_specs = (
        P(None, "vib", None),
        P("ka", "vib", "grp"),
        P("ka", "vib", ("grp", "fin")),
        P(("grp", "ka")),
    )
    out_specs = P(("grp", "ka", "vib"), "fin")
    return jax.shard_map(
        functools.partial(on_device, mesh.shape["ka"]),
        mesh=mesh, in_specs=in_specs, out_specs=out_specs, check_vma=False,
    )
```

```python
import functools

import jax
import jax.numpy as jnp
from jax import lax
from jax.experimental import pallas as pl
from jax.experimental.pallas import tpu as pltpu
from jax.sharding import PartitionSpec as P

JQ = 30
MESH = pl.DeviceIdType.MESH
F32 = jnp.float32
BF16 = jnp.bfloat16


def coefficient_rows(index, width):
    value = jnp.full((1, width), index, jnp.int32).astype(F32)
    jsquare = float(JQ * (JQ + 1))
    norm_j = jnp.sqrt(jnp.full((1, width), jsquare, F32))
    same = value / norm_j
    upper = 0.5 * jnp.sqrt(jsquare - value * (value + 1.0)) / norm_j
    lower = -0.5 * jnp.sqrt(jsquare - value * (value - 1.0)) / norm_j
    return same, upper, lower


def kernel(
    n_ka, n_half, chunks, counts_ref, moments_hbm, initial_hbm, final_hbm, out_ref,
    mom, ini, raw, own, edge, comb, split, amp, part, zsend, zrecv,
    mom_sem, ini_sem, raw_sem, own_send, own_recv, z_send, z_recv,
    fwd_send, fwd_recv, part_send, part_recv, out_send, out_recv,
):
    kblocks, rows, width = raw.shape
    states = ini.shape[2]
    share = out_ref.shape[0]
    whole = mom.shape[2]
    half = width // n_half
    a = lax.axis_index("ka")
    b = lax.axis_index("vib")
    other = 1 - b
    first = a * kblocks - kblocks * n_ka // 2

    get_final = pltpu.make_async_copy(final_hbm, raw, raw_sem)
    get_final.start()
    cores = (b, other)

    def cols_of(core):
        return pl.ds(pl.multiple_of(core * rows, rows), rows)

    def get_moments(i, c):
        span = cols_of(cores[i])
        return pltpu.make_async_copy(
            moments_hbm.at[c, :, span], mom.at[c, :, span], mom_sem.at[i, c]
        )

    for i in range(2):
        for c in range(2):
            get_moments(i, c).start()
    get_initial = pltpu.make_async_copy(initial_hbm, ini, ini_sem)
    get_initial.start()

    barrier = pltpu.get_barrier_semaphore()
    pl.semaphore_signal(barrier, inc=1, device_id={"vib": other}, device_id_type=MESH)
    for d in range(1, n_ka):
        pl.semaphore_signal(
            barrier, inc=1, device_id={"ka": lax.rem(a + d, n_ka)}, device_id_type=MESH
        )

    get_final.wait()
    own_rows = cols_of(b)
    row_index = lax.broadcasted_iota(jnp.int32, (rows, half), 0) + b * rows
    for h in range(n_half):
        for k in range(kblocks):
            live = row_index < counts_ref[k]
            piece = raw[k, :, h * half : (h + 1) * half].astype(F32)
            own[h, own_rows, k * half : (k + 1) * half] = jnp.where(live, piece, 0.0).astype(BF16)

    has_up = a < n_ka - 1
    has_down = a > 0
    pl.semaphore_wait(barrier, n_ka)

    step = rows // chunks

    def at(core, j):
        return pl.ds(pl.multiple_of(core * rows + j * step, step), step)

    def side_lanes(side):
        return pl.ds(side * half, half)

    def z_copy(side, h, j):
        to = a + 1 if side == 0 else a - 1
        return pltpu.make_async_remote_copy(
            src_ref=own.at[h, at(b, j), side_lanes(1 - side)],
            dst_ref=edge.at[h, at(b, j), side_lanes(side)],
            send_sem=z_send.at[side, h, j],
            recv_sem=z_recv.at[side, h, j],
            device_id={"ka": to},
            device_id_type=MESH,
        )

    def forward(side, h, j):
        return pltpu.make_async_remote_copy(
            src_ref=edge.at[h, at(b, j), side_lanes(side)],
            dst_ref=edge.at[h, at(b, j), side_lanes(side)],
            send_sem=fwd_send.at[side, h, j],
            recv_sem=fwd_recv.at[side, h, j],
            device_id={"vib": other},
            device_id_type=MESH,
        )

    def own_copy(h):
        return pltpu.make_async_remote_copy(
            src_ref=own.at[h, own_rows],
            dst_ref=own.at[h, own_rows],
            send_sem=own_send.at[h],
            recv_sem=own_recv.at[h],
            device_id={"vib": other},
            device_id_type=MESH,
        )

    sends = (has_up, has_down)
    takes = (has_down, has_up)
    for h in range(n_half):
        for j in range(chunks):
            for side in range(2):
                @pl.when(sends[side])
                def _():
                    z_copy(side, h, j).start()
        own_copy(h).start()
    for side in range(2):
        @pl.when(jnp.logical_not(takes[side]))
        def _():
            for h in range(n_half):
                edge[h, :, side * half : (side + 1) * half] = jnp.zeros((whole, half), BF16)

    same0, upper0, _ = coefficient_rows(first, half)
    same1, _, lower1 = coefficient_rows(first + 1, half)
    _, upper_below, _ = coefficient_rows(first - 1, half)
    _, _, lower_above = coefficient_rows(first + 2, half)
    same_row = jnp.concatenate([same0, same1], axis=1)
    cross_row = jnp.concatenate([lower1, upper0], axis=1)
    edge_row = jnp.concatenate([upper_below, lower_above], axis=1)

    def relay(h, j):
        for side in range(2):
            @pl.when(takes[side])
            def _():
                z_copy(side, h, j).wait_recv()
                forward(side, h, j).start()

    tile = rows // 2
    for i in range(2):
        for c in range(2):
            get_moments(i, c).wait()
        for h in range(n_half):
            if i == 1:
                own_copy(h).wait_recv()
            piece = own[h, cols_of(cores[i]), :]
            for t in range(2):
                span = pl.ds(t * tile, tile)
                along_z = jnp.dot(
                    mom[0, span, cols_of(cores[i])], piece, preferred_element_type=F32
                )
                along_x = jnp.dot(
                    mom[1, span, cols_of(cores[i])], piece, preferred_element_type=F32
                )
                crossed = jnp.concatenate([along_x[:, half:], along_x[:, :half]], axis=1)
                value = same_row * along_z + cross_row * crossed
                comb[h, span, :] = value if i == 0 else comb[h, span, :] + value

    def take(h, core, j):
        piece = edge[h, at(core, j), :]
        for t in range(2):
            span = pl.ds(t * tile, tile)
            comb[h, span, :] = comb[h, span, :] + edge_row * jnp.dot(
                mom[1, span, at(core, j)], piece, preferred_element_type=F32
            )

    block = min(256, rows)
    lane_index = lax.broadcasted_iota(jnp.int32, (half, block), 1) + b * rows

    def split_half(h):
        for t in range(rows // block):
            both = comb[h, pl.ds(t * block, block), :].T
            for k in range(kblocks):
                turned = both[k * half : (k + 1) * half]
                turned = jnp.where(lane_index + t * block < counts_ref[k], turned, 0.0)
                high = turned.astype(BF16)
                low = (turned - high.astype(F32)).astype(BF16)
                split[h, k, pl.ds(0, half), pl.ds(t * block, block)] = high
                split[h, k, pl.ds(half, half), pl.ds(t * block, block)] = low

    lanes = min(256, states)
    n_blocks = states // lanes
    targets = lanes // (2 * share)
    own_block = a // targets if targets > 1 else a

    toward = 2 * ((2 * a) // n_ka) - 1

    def block_of(s):
        return lax.rem(own_block + toward * (1 + s) + n_blocks, n_blocks)

    def part_copy(h, s):
        size = targets * share
        span = pl.ds(pl.multiple_of(block_of(s) * size, size), size)
        return pltpu.make_async_remote_copy(
            src_ref=amp.at[h, other, span],
            dst_ref=part.at[h, span],
            send_sem=part_send.at[h, s],
            recv_sem=part_recv.at[h, s],
            device_id={"vib": other},
            device_id_type=MESH,
        )

    def out_copy(h, target, slot):
        return pltpu.make_async_remote_copy(
            src_ref=zsend.at[h, slot],
            dst_ref=zrecv.at[h, a],
            send_sem=out_send.at[h, slot],
            recv_sem=out_recv.at[h, a],
            device_id={"ka": target},
            device_id_type=MESH,
        )

    def finish(h, s):
        part_copy(h, s).wait_recv()
        for j in range(targets):
            target = block_of(s) * targets + j
            span = pl.ds(pl.multiple_of(target * share, share), share)
            slot = s * targets + j
            value = amp[h, b, span, :] + part[h, span, :]
            zsend[h, slot] = value

            @pl.when(target == a)
            def _():
                out_ref[:, h * half : (h + 1) * half] = value

            @pl.when(target != a)
            def _():
                out_copy(h, target, slot).start()

    def amplitude_block(h, s):
        cols = pl.ds(pl.multiple_of(block_of(s) * lanes, lanes), lanes)
        both = jnp.dot(split[h, 0], ini[0, :, cols], preferred_element_type=F32)
        for k in range(1, kblocks):
            both = both + jnp.dot(split[h, k], ini[k, :, cols], preferred_element_type=F32)
        value = (both[:half] + both[half:]).T
        for j in range(targets):
            for core in range(2):
                low = (j * 2 + core) * share
                target = block_of(s) * targets + j
                amp[h, core, pl.ds(pl.multiple_of(target * share, share), share), :] = value[
                    low : low + share
                ]
        part_copy(h, s).start()

    for h in range(n_half):
        for j in range(chunks):
            if h == 0 or j > 0:
                relay(h, j)
            take(h, b, j)
        for j in range(chunks):
            for side in range(2):
                @pl.when(takes[side])
                def _():
                    forward(side, h, j).wait_recv()
            take(h, other, j)
        split_half(h)
        if h == 0:
            get_initial.wait()
        for s in range(n_blocks):
            amplitude_block(h, s)
            if s > 0:
                finish(h, s - 1)
            if s == n_blocks // 2 and h + 1 < n_half:
                relay(h + 1, 0)
    for h in range(n_half):
        finish(h, n_blocks - 1)

    for h in range(n_half):
        for d in range(1, n_ka):
            sender = lax.rem(a + d, n_ka)
            pltpu.make_async_remote_copy(
                src_ref=zsend.at[h, 0],
                dst_ref=zrecv.at[h, sender],
                send_sem=out_send.at[h, 0],
                recv_sem=out_recv.at[h, sender],
                device_id={"ka": sender},
                device_id_type=MESH,
            ).wait_recv()
            lanes_h = pl.ds(h * half, half)
            out_ref[:, lanes_h] = out_ref[:, lanes_h] + zrecv[h, sender]

    for h in range(n_half):
        own_copy(h).wait_send()
        for j in range(chunks):
            for side in range(2):
                @pl.when(sends[side])
                def _():
                    z_copy(side, h, j).wait_send()

                @pl.when(takes[side])
                def _():
                    forward(side, h, j).wait_send()
        for s in range(n_blocks):
            part_copy(h, s).wait_send()
            for j in range(targets):
                target = block_of(s) * targets + j

                @pl.when(target != a)
                def _():
                    out_copy(h, target, s * targets + j).wait_send()


def on_device(n_ka, moments, initial_vectors, final_vectors, basis_counts):
    kblocks, rows, states = initial_vectors.shape
    width = final_vectors.shape[2]
    whole = moments.shape[2]
    share = states // (2 * n_ka)
    n_half = max(1, width // 128)
    half = width // n_half
    chunks = 2
    dma = pltpu.SemaphoreType.DMA
    n_blocks = states // min(256, states)
    amplitude = pl.pallas_call(
        functools.partial(kernel, n_ka, n_half, chunks),
        out_shape=jax.ShapeDtypeStruct((share, width), F32),
        in_specs=[pl.BlockSpec(memory_space=pltpu.SMEM)]
        + [pl.BlockSpec(memory_space=pl.ANY)] * 3,
        out_specs=pl.BlockSpec(memory_space=pltpu.VMEM),
        scratch_shapes=[
            pltpu.VMEM(moments.shape, BF16),
            pltpu.VMEM(initial_vectors.shape, BF16),
            pltpu.VMEM(final_vectors.shape, BF16),
            pltpu.VMEM((n_half, whole, kblocks * half), BF16),
            pltpu.VMEM((n_half, whole, 2 * half), BF16),
            pltpu.VMEM((n_half, rows, kblocks * half), F32),
            pltpu.VMEM((n_half, kblocks, 2 * half, rows), BF16),
            pltpu.VMEM((n_half, 2, n_ka * share, half), F32),
            pltpu.VMEM((n_half, n_ka * share, half), F32),
            pltpu.VMEM((n_half, n_ka, share, half), F32),
            pltpu.VMEM((n_half, n_ka, share, half), F32),
            dma((2, 2)),
            dma(()),
            dma(()),
            dma((n_half,)),
            dma((n_half,)),
            dma((2, n_half, chunks)),
            dma((2, n_half, chunks)),
            dma((2, n_half, chunks)),
            dma((2, n_half, chunks)),
            dma((n_half, n_blocks)),
            dma((n_half, n_blocks)),
            dma((n_half, n_ka)),
            dma((n_half, n_ka)),
        ],
        compiler_params=pltpu.CompilerParams(
            collective_id=0, has_side_effects=True, vmem_limit_bytes=60 * 2**20
        ),
    )(basis_counts, moments, initial_vectors, final_vectors)
    return amplitude * amplitude


def solution(mesh):
    in_specs = (
        P(None, "vib", None),
        P("ka", "vib", "grp"),
        P("ka", "vib", ("grp", "fin")),
        P(("grp", "ka")),
    )
    out_specs = P(("grp", "ka", "vib"), "fin")
    return jax.shard_map(
        functools.partial(on_device, mesh.shape["ka"]),
        mesh=mesh, in_specs=in_specs, out_specs=out_specs, check_vma=False,
    )
```
